128 devices in a mesh: group: 2 (over y_hi), shard: 64 (over y_lo, z, x, core).
Axes of the slice: x: 4, y: 4 (y_hi: 2, y_lo: 2; y = y_hi * 2 + y_lo), z: 4, core: 2. Of those that a mesh axis runs over, the one named last changes fastest.
Arguments:
- image_tokens: bfloat16 [256, 256, 2432], P(('group', 'shard')), may hold values from -6 to 6
- image_gain: float32 [2432], replicated, may hold values from 0.1 to 1.9
- caption_states: bfloat16 [256, 384, 2432], P('group', None, 'shard'), may hold values from -6 to 6
- text_gain: float32 [2432], replicated, may hold values from 0.1 to 1.9
- lengths: int32 [2, 128], P('group'), may hold values from 1 to 333, as said below
- assign: int32 [2, 128], P('group'), may hold values from 0 to 127, as said below
- image_qkv: bfloat16 [2432, 3840], P(('group', 'shard')), may hold values from -0.125 to 0.125
- text_kv: bfloat16 [2432, 2560], P(('group', 'shard')), may hold values from -0.125 to 0.125
Outputs:
- attended: bfloat16 [256, 256, 1280], P(('group', 'shard'))
The draws below stay inside these ranges and needn't reach their ends.
Inputs may be any that keep to these rules, and one draw needn't show every extreme that they name: Each row is a permutation: a half's trainer slots assign[g, s], 2 consecutive slots to each device of the half in order. `lengths`: caption rows at or beyond a sample's length are padding and take no part in attention. Counting ceil(length / 128) blocks of 128 rows for each sample, the 2 samples of one trainer device use exactly 4 blocks together.
All inputs are finite; a program needn't handle non-finite values.
Results may differ from the reference program's by a relative error of at most 0.0083.
Values may be sent and summed in bfloat16 or wider, within the bound.
A program may use at most 192 MiB of HBM per device.

```python
import jax
import jax.numpy as jnp
from jax import lax

D = 2432
HD = 64
HEADS = 20
IMG = 256
TXT = 384
BLK = 128
LEN_MAX = 333
HW = 1280
SAMP_G = 128
SAMPLES = 256
N_GROUP = 2


def joint_draw(key):
    base = jax.random.fold_in(key, 4242)
    key_blocks = jax.random.fold_in(base, 1)
    key_lengths = jax.random.fold_in(base, 2)
    key_perm = jax.random.fold_in(base, 3)
    nb = (LEN_MAX + BLK - 1) // BLK
    pairs = SAMP_G // 2
    first = jax.random.randint(key_blocks, (N_GROUP, pairs), 1, nb + 1).astype(jnp.int32)
    first = first.at[:, 0].set(nb)
    blocks = jnp.stack([first, nb + 1 - first], axis=-1).reshape(N_GROUP, SAMP_G)
    low = (blocks - 1) * BLK
    high = jnp.minimum(blocks * BLK, LEN_MAX)
    raw = jax.random.randint(key_lengths, (N_GROUP, SAMP_G), 0, 1 << 20).astype(jnp.int32)
    slot_len = low + 1 + raw % (high - low)
    slot_len = slot_len.at[:, 0].set(LEN_MAX)
    slot_len = slot_len.at[:, 1].set(1)
    keys = jax.random.split(key_perm, N_GROUP)
    assign = jax.vmap(lambda one: jax.random.permutation(one, SAMP_G))(keys).astype(jnp.int32)
    lengths = jnp.take_along_axis(slot_len, assign, axis=1).astype(jnp.int32)
    return (lengths, assign)


def draw_lengths(key, part):
    return joint_draw(key)[0]


def draw_assign(key, part):
    return joint_draw(key)[1]


def block_levels(rng, shape, cuts, smallest, largest):
    def one(position, blocks):
        draws = jax.random.uniform(jax.random.fold_in(jax.random.fold_in(rng, 6), position), (blocks,), jnp.float32, smallest / len(cuts), largest / len(cuts))
        return jnp.repeat(jnp.exp(draws), shape[position] // blocks).reshape((-1,) + (1,) * (len(shape) - position - 1))

    level = one(*cuts[0])
    for cut in cuts[1:]:
        level = level * one(*cut)
    return level


def centred(key, extent, scale, reach, shards=(), kind=jnp.bfloat16):
    result = scale * jax.random.normal(key, extent, jnp.float32)
    if shards:
        result = result * block_levels(key, extent, shards, -0.22, 0.18)
    return jnp.clip(result, -reach, reach).astype(kind)


def setup_inputs(seed: int = 0) -> dict:
    splits = jax.random.split(jax.random.key(seed), 9)
    image_tokens = centred(splits[0], (SAMPLES, IMG, D), 1.0, 6.0, ((0, 128),))
    image_gain = jnp.clip(1.0 + 0.18 * jax.random.normal(splits[1], (D,), jnp.float32), 0.1, 1.9)
    caption_states = centred(splits[2], (SAMPLES, TXT, D), 1.0, 6.0, ((0, 2), (2, 64)))
    text_gain = jnp.clip(1.0 + 0.18 * jax.random.normal(splits[3], (D,), jnp.float32), 0.1, 1.9)
    lengths = draw_lengths(jax.random.fold_in(splits[8], 71), 0)
    assign = draw_assign(jax.random.fold_in(splits[8], 71), 0)
    image_qkv = centred(splits[6], (D, 3 * HW), D ** -0.5, 0.125, ((0, 128),))
    text_kv = centred(splits[7], (D, 2 * HW), D ** -0.5, 0.125, ((0, 128),))
    return dict(image_tokens=image_tokens, image_gain=image_gain, caption_states=caption_states, text_gain=text_gain, lengths=lengths, assign=assign, image_qkv=image_qkv, text_kv=text_kv)


def layer_norm(rows, gain):
    values = rows.astype(jnp.float32)
    mean = lax.optimization_barrier(jnp.mean(values, axis=-1, keepdims=True))
    var = lax.optimization_barrier(jnp.mean((values - mean) ** 2, axis=-1, keepdims=True))
    return ((values - mean) * lax.rsqrt(var + 1e-06) * gain).astype(jnp.bfloat16)

def head_norm(values):
    return values * lax.rsqrt(lax.optimization_barrier(jnp.mean(values * values, axis=-1, keepdims=True)) + 1e-06)

def one_sample(image_rows, caption_rows, length, image_gain, text_gain, image_qkv, text_kv):
    image_normed = layer_norm(image_rows, image_gain)
    text_normed = layer_norm(caption_rows, text_gain)
    image_proj = jnp.dot(image_normed, image_qkv, preferred_element_type=jnp.float32)
    text_proj = jnp.dot(text_normed, text_kv, preferred_element_type=jnp.float32)
    width = HEADS * HD
    query = head_norm(image_proj[:, :width].reshape(IMG, HEADS, HD)).astype(jnp.bfloat16)
    key_img = head_norm(image_proj[:, width:2 * width].reshape(IMG, HEADS, HD)).astype(jnp.bfloat16)
    val_img = image_proj[:, 2 * width:].reshape(IMG, HEADS, HD).astype(jnp.bfloat16)
    key_txt = head_norm(text_proj[:, :width].reshape(TXT, HEADS, HD)).astype(jnp.bfloat16)
    val_txt = text_proj[:, width:].reshape(TXT, HEADS, HD).astype(jnp.bfloat16)
    scale = HD ** (-0.5)
    query_f = query.astype(jnp.float32)
    score_img = jnp.einsum('qhd,khd->hqk', query_f, key_img.astype(jnp.float32)) * scale
    score_txt = jnp.einsum('qhd,khd->hqk', query_f, key_txt.astype(jnp.float32)) * scale
    valid = jnp.arange(TXT) < length
    score_txt = jnp.where(valid[None, None, :], score_txt, -1e+30)
    top = jnp.maximum(lax.optimization_barrier(jnp.max(score_img, axis=-1, keepdims=True)), lax.optimization_barrier(jnp.max(score_txt, axis=-1, keepdims=True)))
    prob_img = jnp.exp(score_img - top)
    prob_txt = jnp.exp(score_txt - top)
    total = lax.optimization_barrier(jnp.sum(prob_img, axis=-1)) + lax.optimization_barrier(jnp.sum(prob_txt, axis=-1))
    prob_img = prob_img.astype(jnp.bfloat16).astype(jnp.float32)
    prob_txt = prob_txt.astype(jnp.bfloat16).astype(jnp.float32)
    mixed = jnp.einsum('hqk,khd->qhd', prob_img, val_img.astype(jnp.float32))
    mixed = mixed + jnp.einsum('hqk,khd->qhd', prob_txt, val_txt.astype(jnp.float32))
    mixed = mixed / jnp.transpose(total)[:, :, None]
    return mixed.reshape(IMG, HEADS * HD).astype(jnp.bfloat16)

def reference(image_tokens, image_gain, caption_states, text_gain, lengths, assign, image_qkv, text_kv):
    groups = assign.shape[0]
    count = assign.shape[1]
    places = jnp.arange(count, dtype=jnp.int32)
    match = (assign[:, :, None] == places[None, None, :]).astype(jnp.int32)
    inverse = lax.optimization_barrier(jnp.sum(match * places[None, :, None], axis=1)).astype(jnp.int32)
    source = (inverse + (jnp.arange(groups, dtype=jnp.int32) * count)[:, None]).reshape(-1)
    flat_lengths = lengths.reshape(-1)

    def run(slot):
        anchor = source[slot]
        return one_sample(image_tokens[slot], caption_states[anchor], flat_lengths[anchor], image_gain, text_gain, image_qkv, text_kv)
    return lax.map(run, jnp.arange(groups * count, dtype=jnp.int32))
```

```python
import functools

import jax
import jax.numpy as jnp
from jax import lax
from jax.experimental import pallas as pl
from jax.experimental.pallas import tpu as pltpu
from jax.sharding import Mesh, PartitionSpec as P

D = 2432
HW = 1280
FEAT = 38
PADF = 40
CHIPS = 64
DP = CHIPS * PADF
PAIRS = 5
ROWS = 512
HALF = 640
AXES = ("yh", "yl", "z", "x", "c")
CHIP_AXES = ("yh", "yl", "z", "x")
SHARD_AXES = ("yl", "z", "x", "c")
f32 = jnp.float32
bf16 = jnp.bfloat16


def compact_kernel(src_ref, blk_ref, x_ref, o_ref, sem):
    def copy(e):
        b = pl.multiple_of(blk_ref[e] * 128, 128)
        return pltpu.make_async_copy(
            x_ref.at[src_ref[e], :, pl.ds(b, 128)], o_ref.at[e], sem
        )

    @pl.loop(0, 256)
    def _(e):
        copy(e).start()

    pltpu.make_async_copy(o_ref, o_ref, sem).wait()


def compact(caps, src, blk):
    return pl.pallas_call(
        compact_kernel,
        out_shape=jax.ShapeDtypeStruct((256, PADF, 128), bf16),
        grid_spec=pltpu.PrefetchScalarGridSpec(
            num_scalar_prefetch=2,
            grid=(1,),
            in_specs=[pl.BlockSpec((128, PADF, 384), lambda i, a, b: (0, 0, 0))],
            out_specs=pl.BlockSpec(memory_space=pl.ANY),
            scratch_shapes=[pltpu.SemaphoreType.DMA],
        ),
        name="compact",
    )(src, blk, caps)


def layer_norm_rows(x, mask, gain):
    mean = jnp.sum(x, axis=1, keepdims=True) * (1.0 / D)
    d = x - mean
    if mask is not None:
        d = d * mask
    var = jnp.sum(d * d, axis=1, keepdims=True) * (1.0 / D)
    return (d * lax.rsqrt(var + 1e-06) * gain).astype(bf16)


def spread_block(o):
    first = 128 * o
    start = (first // PADF) * FEAT + min(first % PADF, FEAT)
    lo = min(start // 128 * 128, D - 256)
    r = lax.broadcasted_iota(jnp.int32, (256, 128), 0)
    col = lax.broadcasted_iota(jnp.int32, (256, 128), 1) + first
    blk = lax.div(col, PADF)
    off = col - blk * PADF
    hit = (r + lo == blk * FEAT + off) & (off < FEAT)
    return lo, jnp.where(hit, 1.0, 0.0).astype(bf16)


def image_kernel(x_ref, g_ref, o_ref):
    y = layer_norm_rows(x_ref[...].astype(f32), None, g_ref[...])
    for o in range(DP // 128):
        lo, s = spread_block(o)
        o_ref[:, 128 * o : 128 * o + 128] = jnp.dot(
            y[:, lo : lo + 256], s, preferred_element_type=f32
        ).astype(bf16)


def image_prep(x, gain):
    return pl.pallas_call(
        image_kernel,
        out_shape=jax.ShapeDtypeStruct((ROWS, DP), bf16),
        grid=(4,),
        in_specs=[
            pl.BlockSpec((128, D), lambda i: (i, 0)),
            pl.BlockSpec((1, D), lambda i: (0, 0)),
        ],
        out_specs=pl.BlockSpec((128, DP), lambda i: (i, 0)),
        cost_estimate=pl.CostEstimate(
            flops=2 * ROWS * 256 * DP, bytes_accessed=4 * ROWS * DP, transcendentals=0
        ),
        name="image_prep",
    )(x, gain.reshape(1, D))


def text_kernel(x_ref, g_ref, m_ref, o_ref):
    x = x_ref[:, 0].reshape(DP, 128)
    o_ref[...] = layer_norm_rows(
        jnp.transpose(x.astype(f32)), m_ref[...], g_ref[...]
    )


def text_prep(x, gain_row, mask_row):
    return pl.pallas_call(
        text_kernel,
        out_shape=jax.ShapeDtypeStruct((ROWS, DP), bf16),
        grid=(4,),
        in_specs=[
            pl.BlockSpec((CHIPS, 1, PADF, 128), lambda i: (0, i, 0, 0)),
            pl.BlockSpec((1, DP), lambda i: (0, 0)),
            pl.BlockSpec((1, DP), lambda i: (0, 0)),
        ],
        out_specs=pl.BlockSpec((128, DP), lambda i: (i, 0)),
        cost_estimate=pl.CostEstimate(
            flops=8 * ROWS * DP, bytes_accessed=4 * ROWS * DP, transcendentals=0
        ),
        name="text_prep",
    )(x, gain_row, mask_row)


def head_scale(y, ones):
    sq = y * y
    hi = sq.astype(bf16)
    lo = (sq - hi.astype(f32)).astype(bf16)
    total = jnp.dot(hi, ones, preferred_element_type=f32) + jnp.dot(
        lo, ones, preferred_element_type=f32
    )
    return y * lax.rsqrt(total * (1.0 / 64.0) + 1e-06)


def main_kernel(len_ref, x_ref, t_ref, w_ref, o_ref, q_s, k_s, v_s, tk_s, tv_s):
    def weights(i):
        return w_ref[:, i].reshape(DP, 128)

    a = lax.broadcasted_iota(jnp.int32, (256, 256), 0) // 64
    b = lax.broadcasted_iota(jnp.int32, (256, 256), 1) // 64
    ones = jnp.where(a == b, 1.0, 0.0).astype(bf16)

    qk = jnp.dot(
        x_ref[...],
        jnp.concatenate([weights(0), weights(1)], axis=1),
        preferred_element_type=f32,
    )
    qk = head_scale(qk, ones)
    q_s[...] = (qk[:, :128] * 0.125).astype(bf16)
    k_s[...] = qk[:, 128:].astype(bf16)
    v_s[...] = jnp.dot(x_ref[...], weights(2), preferred_element_type=f32).astype(bf16)
    tkv = jnp.dot(
        t_ref[...],
        jnp.concatenate([weights(3), weights(4)], axis=1),
        preferred_element_type=f32,
    )
    tk_s[...] = head_scale(tkv[:, :128], ones[:128, :128]).astype(bf16)
    tv_s[...] = tkv[:, 128:].astype(bf16)

    left = lax.broadcasted_iota(jnp.int32, (640, 128), 1) < 64
    zero = jnp.zeros((640, 128), bf16)
    one = jnp.ones((640, 128), bf16)
    row = lax.broadcasted_iota(jnp.int32, (384, 128), 0)

    for s in range(4):
        dev, j = s // 2, s % 2
        base = dev * ROWS + j * 128
        if j == 0:
            pos = row
        else:
            pos = (2 - row // 128) * 128 + row % 128
        live = pos < len_ref[s]
        q = q_s[pl.ds(s * 256, 256), :]
        k = jnp.concatenate(
            [k_s[pl.ds(s * 256, 256), :], tk_s[pl.ds(base, 384), :]], axis=0
        )
        v = jnp.concatenate(
            [
                v_s[pl.ds(s * 256, 256), :],
                jnp.where(live, tv_s[pl.ds(base, 384), :], 0).astype(bf16),
            ],
            axis=0,
        )
        n = jnp.concatenate(
            [one[:256], jnp.where(live, 1.0, 0.0).astype(bf16)], axis=0
        )
        kk = jnp.concatenate(
            [jnp.where(left, k, zero), jnp.where(left, zero, k)], axis=0
        )
        sc = lax.dot_general(
            q, kk, (((1,), (1,)), ((), ())), preferred_element_type=f32
        )
        p = jnp.exp(sc).astype(bf16)
        vv = jnp.concatenate(
            [
                jnp.concatenate([jnp.where(left, v, zero), jnp.where(left, n, zero)], 1),
                jnp.concatenate([jnp.where(left, zero, v), jnp.where(left, zero, n)], 1),
            ],
            axis=0,
        )
        o = jnp.dot(p, vv, preferred_element_type=f32)
        o_ref[pl.ds(s * 256, 256), :] = (o[:, :128] / o[:, 128:]).astype(bf16)


def main(lens, x, t, w):
    return pl.pallas_call(
        main_kernel,
        out_shape=jax.ShapeDtypeStruct((2 * ROWS, HALF), bf16),
        grid_spec=pltpu.PrefetchScalarGridSpec(
            num_scalar_prefetch=1,
            grid=(PAIRS,),
            in_specs=[
                pl.BlockSpec((2 * ROWS, DP), lambda i, a: (0, 0)),
                pl.BlockSpec((2 * ROWS, DP), lambda i, a: (0, 0)),
                pl.BlockSpec((CHIPS, 5, PADF, 128), lambda i, a: (0, i, 0, 0)),
            ],
            out_specs=pl.BlockSpec((2 * ROWS, 128), lambda i, a: (0, i)),
            scratch_shapes=[pltpu.VMEM((2 * ROWS, 128), bf16)] * 5,
        ),
        cost_estimate=pl.CostEstimate(
            flops=2 * 2 * ROWS * DP * 5 * 640,
            bytes_accessed=2 * DP * 3200 + 8 * ROWS * DP,
            transcendentals=4 * 2560 * 2560,
        ),
        compiler_params=pltpu.CompilerParams(vmem_limit_bytes=60 << 20),
        name="proj_attend",
    )(lens, x, t, w)


def chip_weights(image_qkv, text_kv, core):
    wi = image_qkv.reshape(19, 3, 2, PAIRS, 128)
    wt = text_kv.reshape(19, 2, 2, PAIRS, 128)
    w = jnp.concatenate([wi, wt], axis=1).transpose(2, 3, 1, 0, 4)
    w = w.reshape(2, 25, 19, 128)
    w = jnp.where(
        core == 0,
        jnp.pad(w, ((0, 0), (0, 0), (0, 21), (0, 0))),
        jnp.pad(w, ((0, 0), (0, 0), (19, 2), (0, 0))),
    )
    mine = jnp.where(core == 0, w[0], w[1])
    other = jnp.where(core == 0, w[1], w[0])
    return mine + lax.ppermute(other, "c", [(0, 1), (1, 0)])


def shards(
    image_tokens, image_gain, caption_states, text_gain, lengths, assign, image_qkv, text_kv
):
    core = lax.axis_index("c")
    chip = lax.axis_index(("yl", "z", "x"))

    w = lax.all_gather(chip_weights(image_qkv, text_kv, core), CHIP_AXES, axis=0)

    places = jnp.arange(128, dtype=jnp.int32)
    match = assign[0][:, None] == places[None, :]
    inverse = jnp.sum(jnp.where(match, places[:, None], 0), axis=0)
    ordered = jnp.sum(jnp.where(match, lengths[0][:, None], 0), axis=0)
    pair_src = inverse.reshape(64, 2)
    first = (ordered.reshape(64, 2)[:, :1] + 127) // 128
    slot = jnp.arange(4, dtype=jnp.int32)[None, :]
    own = slot < first
    src = jnp.where(own, pair_src[:, :1], pair_src[:, 1:]).reshape(256)
    blk = jnp.clip(jnp.where(own, slot, 3 - slot), 0, 2).reshape(256)
    lens = lax.dynamic_slice_in_dim(ordered, chip * 4, 4, 0)

    caps = jnp.pad(jnp.transpose(caption_states, (0, 2, 1)), ((0, 0), (0, 2), (0, 0)))
    caps = compact(caps, src, blk).reshape(64, 4, PADF, 128)
    caps = lax.all_to_all(caps, SHARD_AXES, split_axis=0, concat_axis=0, tiled=True)

    def spread_row(v):
        return jnp.pad(v.reshape(CHIPS, FEAT), ((0, 0), (0, 2))).reshape(1, DP)

    mask_row = spread_row(jnp.ones((D,), f32))
    t = text_prep(caps, spread_row(text_gain), mask_row)
    x = image_prep(image_tokens.reshape(ROWS, D), image_gain)
    x = lax.all_gather(x, "c", axis=0, tiled=True)
    t = lax.all_gather(t, "c", axis=0, tiled=True)
    out = main(lens, x, t, w)
    out = lax.all_to_all(
        out.reshape(2, ROWS, HALF), "c", split_axis=0, concat_axis=0, tiled=True
    )
    return jnp.concatenate([out[0], out[1]], axis=1).reshape(2, 256, HW)


def solution(mesh):
    fine = Mesh(mesh.devices.reshape(2, 2, 4, 4, 2), AXES)
    full = P(AXES)
    placed = (
        P(AXES, None, None),
        P(),
        P("yh", None, SHARD_AXES),
        P(),
        P("yh", None),
        P("yh", None),
        P(AXES, None),
        P(AXES, None),
    )
    return jax.shard_map(
        shards,
        mesh=fine,
        in_specs=placed,
        out_specs=P(AXES, None, None),
        check_vma=False,
    )
```

```python
import functools

import jax
import jax.numpy as jnp
from jax import lax
from jax.experimental import pallas as pl
from jax.experimental.pallas import tpu as pltpu
from jax.sharding import Mesh, PartitionSpec as P

D = 2432
HW = 1280
FEAT = 38
PADF = 40
CHIPS = 64
DP = CHIPS * PADF
PAIRS = 5
ROWS = 512
HALF = 640
AXES = ("yh", "yl", "z", "x", "c")
CHIP_AXES = ("yh", "yl", "z", "x")
SHARD_AXES = ("yl", "z", "x", "c")
f32 = jnp.float32
bf16 = jnp.bfloat16


DIMS = (("x", "z", "y"), ("z", "y", "x"), ("y", "x", "z"))
STEPS = 9
MESH = pl.DeviceIdType.MESH


def layer_norm_rows(x, mask, gain):
    mean = jnp.sum(x, axis=1, keepdims=True) * (1.0 / D)
    d = x - mean
    if mask is not None:
        d = d * mask
    var = jnp.sum(d * d, axis=1, keepdims=True) * (1.0 / D)
    return (d * lax.rsqrt(var + 1e-06) * gain).astype(bf16)


def spread_low(o):
    first = 128 * o
    start = (first // PADF) * FEAT + min(first % PADF, FEAT)
    return min(start // 128 * 128, D - 256)


def spread_block(o):
    first = 128 * o
    lo = spread_low(o)
    r = lax.broadcasted_iota(jnp.int32, (256, 128), 0)
    col = lax.broadcasted_iota(jnp.int32, (256, 128), 1) + first
    blk = lax.div(col, PADF)
    off = col - blk * PADF
    hit = (r + lo == blk * FEAT + off) & (off < FEAT)
    return lo, jnp.where(hit, 1.0, 0.0).astype(bf16)


def head_scale(y, ones):
    sq = y * y
    hi = sq.astype(bf16)
    lo = (sq - hi.astype(f32)).astype(bf16)
    total = jnp.dot(hi, ones, preferred_element_type=f32) + jnp.dot(
        lo, ones, preferred_element_type=f32
    )
    return y * lax.rsqrt(total * (1.0 / 64.0) + 1e-06)


def attend(len_ref, s, q_s, k_s, v_s, tk_s, tv_s):
    left = lax.broadcasted_iota(jnp.int32, (640, 128), 1) < 64
    zero = jnp.zeros((640, 128), bf16)
    row = lax.broadcasted_iota(jnp.int32, (384, 128), 0)
    dev, j = s // 2, s % 2
    base = dev * ROWS + j * 128
    pos = row if j == 0 else (2 - row // 128) * 128 + row % 128
    live = pos < len_ref[s]
    q = q_s[pl.ds(s * 256, 256), :]
    k = jnp.concatenate(
        [k_s[pl.ds(s * 256, 256), :], tk_s[pl.ds(base, 384), :]], axis=0
    )
    v = jnp.concatenate(
        [
            v_s[pl.ds(s * 256, 256), :],
            jnp.where(live, tv_s[pl.ds(base, 384), :], 0).astype(bf16),
        ],
        axis=0,
    )
    n = jnp.concatenate(
        [jnp.ones((256, 128), bf16), jnp.where(live, 1.0, 0.0).astype(bf16)], axis=0
    )
    kk = jnp.concatenate([jnp.where(left, k, zero), jnp.where(left, zero, k)], axis=0)
    sc = lax.dot_general(q, kk, (((1,), (1,)), ((), ())), preferred_element_type=f32)
    p = jnp.exp(sc).astype(bf16)
    vv = jnp.concatenate(
        [
            jnp.concatenate([jnp.where(left, v, zero), jnp.where(left, n, zero)], 1),
            jnp.concatenate([jnp.where(left, zero, v), jnp.where(left, zero, n)], 1),
        ],
        axis=0,
    )
    o = jnp.dot(p, vv, preferred_element_type=f32)
    return (o[:, :128] / o[:, 128:]).astype(bf16)


def fused_kernel(
    src_ref, blk_ref, len_ref, u_hbm, caps_hbm, img_hbm, ig_ref, tg_ref, tm_ref,
    out_hbm,
    w, caps, cc, land, img, xs, ts, spread, o_s, q_s, k_s, v_s, tk_s, tv_s,
    in_sem, s12, r12, s3, r3, a2a_s, a2a_r, px_s, px_r, po_s, po_r, po_l,
):
    yh, yl, z, x, c = (lax.axis_index(a) for a in AXES)
    y = yh * 2 + yl
    at = {"y": y, "z": z, "x": x}

    def device(y_, z_, x_, c_):
        return (y_ // 2, y_ % 2, z_, x_, c_)

    def ring(dim, delta):
        pos = dict(at)
        pos[dim] = (pos[dim] + delta) % 4
        return device(pos["y"], pos["z"], pos["x"], c)

    partner = device(y, z, x, 1 - c)

    def view(phase, color, idx, part=None, a=None):
        count = 9 if color == 0 else 8
        if phase == 2:
            sub = slice(None) if part is None else pl.ds(2 * part, 2)
            if color == 0:
                return w.at[a, 0, idx, sub]
            if color == 1:
                return w.at[a, 1, sub, :, idx]
            return w.at[a, 2, sub, idx]
        if part is None:
            rows = pl.ds(0, count)
        elif part == 0:
            rows = pl.ds(0, (count + 1) // 2)
        else:
            rows = pl.ds((count + 1) // 2, count // 2)
        if phase == 0:
            if color == 0:
                return w.at[rows, 0, y, z, idx]
            if color == 1:
                return w.at[rows, 1, y, idx, x]
            return w.at[rows, 2, idx, z, x]
        if color == 0:
            return w.at[rows, 0, y, idx]
        if color == 1:
            return w.at[rows, 1, idx, :, x]
        return w.at[rows, 2, :, z, idx]

    def message(phase, color, kind, a, shift, part):
        dim = DIMS[color][phase]
        block = view(phase, color, (at[dim] + shift) % 4, part, a)
        if phase == 2:
            send, recv = s3.at[a, color, kind], r3.at[a, color, kind]
        else:
            send, recv = s12.at[phase, color, kind], r12.at[phase, color, kind]
        return pltpu.make_async_remote_copy(
            src_ref=block,
            dst_ref=block,
            send_sem=send,
            recv_sem=recv,
            device_id=ring(dim, 1 if kind % 2 == 0 else -1),
            device_id_type=MESH,
        )

    out_shift = (0, 0, 3, 1)
    in_shift = (3, 1, 2, 2)
    parts = (None, None, 0, 1)

    def each_color(phase, a, f):
        if phase == 2:
            f(0)

            @pl.when(a < 8)
            def _():
                f(1)
                f(2)
        else:
            for color in range(3):
                f(color)

    def send(phase, step, a=None):
        def f(color):
            for kind in (2 * step, 2 * step + 1):
                message(phase, color, kind, a, out_shift[kind], parts[kind]).start()

        each_color(phase, a, f)

    def arrive(phase, step, a=None):
        def f(color):
            for kind in (2 * step, 2 * step + 1):
                message(phase, color, kind, a, in_shift[kind], parts[kind]).wait_recv()

        each_color(phase, a, f)

    def sent(phase, a=None):
        def f(color):
            for kind in range(4):
                message(phase, color, kind, a, out_shift[kind], parts[kind]).wait_send()

        each_color(phase, a, f)

    def advance(a):
        @pl.when(a < STEPS)
        def _():
            arrive(2, 0, a)
            send(2, 1, a)

        @pl.when(a + 2 < STEPS)
        def _():
            send(2, 0, a + 2)

    load_u = pltpu.make_async_copy(u_hbm, w.at[:, :, y, z, x], in_sem.at[0])
    load_caps = pltpu.make_async_copy(caps_hbm, caps, in_sem.at[1])
    load_img = pltpu.make_async_copy(img_hbm, img, in_sem.at[2])
    load_u.start()
    load_caps.start()
    load_img.start()

    me = (yl * 16 + z * 4 + x) * 2 + c

    def peer(k):
        j = (me + k) % 64
        return j, (yh, j // 32, (j // 8) % 4, (j // 2) % 4, j % 2)

    barrier = pltpu.get_barrier_semaphore()

    @pl.loop(1, 64)
    def _(k):
        pl.semaphore_signal(barrier, inc=1, device_id=peer(k)[1], device_id_type=MESH)

    across = (1 - yh, 1 - yl, z, x, c)
    pl.semaphore_signal(barrier, inc=1, device_id=across, device_id_type=MESH)

    for o in range(DP // 128):
        spread[o] = spread_block(o)[1]
    load_u.wait()
    pl.semaphore_wait(barrier, 64)

    send(0, 0)

    load_caps.wait()

    @pl.loop(0, 64)
    def _(d):
        for i in range(4):
            e = d * 4 + i
            b = blk_ref[e]
            rows = caps[src_ref[e]]
            cc[d, i, pl.ds(0, FEAT), :] = jnp.where(
                b == 0,
                rows[:, :128],
                jnp.where(b == 1, rows[:, 128:256], rows[:, 256:]),
            )
            cc[d, i, pl.ds(FEAT, 2), :] = jnp.zeros((2, 128), bf16)

    def exchange(k):
        j, dev = peer(k)
        return pltpu.make_async_remote_copy(
            src_ref=cc.at[j],
            dst_ref=land.at[me],
            send_sem=a2a_s,
            recv_sem=a2a_r,
            device_id=dev,
            device_id_type=MESH,
        )

    keep = pltpu.make_async_copy(cc.at[me], land.at[me], in_sem.at[3])
    keep.start()

    @pl.loop(1, 64)
    def _(k):
        exchange(k).start()

    arrive(0, 0)
    send(0, 1)
    load_img.wait()

    def image_chunk(i):
        rows = pl.ds(i * 128, 128)
        y_n = layer_norm_rows(img[rows, :].astype(f32), None, ig_ref[...])
        for o in range(DP // 128):
            lo = spread_low(o)
            xs[c, rows, 128 * o : 128 * o + 128] = jnp.dot(
                y_n[:, lo : lo + 256], spread[o], preferred_element_type=f32
            ).astype(bf16)

    @pl.loop(0, 2)
    def _(i):
        image_chunk(i)

    arrive(0, 1)
    send(1, 0)

    @pl.loop(2, 4)
    def _(i):
        image_chunk(i)

    def hand_over(buf, n):
        return pltpu.make_async_remote_copy(
            src_ref=buf.at[c],
            dst_ref=buf.at[c],
            send_sem=px_s.at[n],
            recv_sem=px_r.at[n],
            device_id=partner,
            device_id_type=MESH,
        )

    def take_over(buf, n):
        return pltpu.make_async_remote_copy(
            src_ref=buf.at[1 - c],
            dst_ref=buf.at[1 - c],
            send_sem=px_s.at[n],
            recv_sem=px_r.at[n],
            device_id=partner,
            device_id_type=MESH,
        )

    hand_over(xs, 0).start()
    arrive(1, 0)
    send(1, 1)
    arrive(1, 1)
    send(2, 0, 0)
    send(2, 0, 1)

    keep.wait()
    others = land.at[pl.ds(0, 63)]
    pltpu.make_async_copy(others, others, a2a_r).wait()

    @pl.loop(0, 4)
    def _(i):
        raw = land[:, i].reshape(DP, 128)
        ts[c, pl.ds(i * 128, 128), :] = layer_norm_rows(
            jnp.transpose(raw.astype(f32)), tm_ref[...], tg_ref[...]
        )

    hand_over(ts, 1).start()
    advance(0)
    advance(1)
    take_over(xs, 0).wait_recv()
    take_over(ts, 1).wait_recv()

    a_ = lax.broadcasted_iota(jnp.int32, (256, 256), 0) // 64
    b_ = lax.broadcasted_iota(jnp.int32, (256, 256), 1) // 64
    ones = jnp.where(a_ == b_, 1.0, 0.0).astype(bf16)

    def own_part(p):
        cols = pl.ds(pl.multiple_of(c * HALF + p * 128, 128), 128)
        return pltpu.make_async_copy(o_s.at[p, c], out_hbm.at[:, cols], po_l.at[p])

    def their_part(p, core):
        cols = pl.ds(pl.multiple_of(core * HALF + p * 128, 128), 128)
        return pltpu.make_async_remote_copy(
            src_ref=o_s.at[p, 1 - c],
            dst_ref=out_hbm.at[:, cols],
            send_sem=po_s.at[p],
            recv_sem=po_r.at[p],
            device_id=partner,
            device_id_type=MESH,
        )

    @pl.loop(0, PAIRS)
    def _(p):
        def weights(i):
            n = p * 5 + i
            return w[n // 3, n % 3].reshape(DP, 128)

        arrive(2, 1, 2 * p)

        @pl.when(2 * p + 1 < STEPS)
        def _():
            arrive(2, 1, 2 * p + 1)

        act = xs[...].reshape(2 * ROWS, DP)
        qk = jnp.dot(
            act,
            jnp.concatenate([weights(0), weights(1)], axis=1),
            preferred_element_type=f32,
        )
        qk = head_scale(qk, ones)
        q_s[...] = (qk[:, :128] * 0.125).astype(bf16)
        k_s[...] = qk[:, 128:].astype(bf16)
        advance(2 * p + 2)
        v_s[...] = jnp.dot(act, weights(2), preferred_element_type=f32).astype(bf16)
        tkv = jnp.dot(
            ts[...].reshape(2 * ROWS, DP),
            jnp.concatenate([weights(3), weights(4)], axis=1),
            preferred_element_type=f32,
        )
        tk_s[...] = head_scale(tkv[:, :128], ones[:128, :128]).astype(bf16)
        tv_s[...] = tkv[:, 128:].astype(bf16)
        advance(2 * p + 3)
        for s in range(4):
            o_s[p, s // 2, pl.ds(s % 2 * 256, 256), :] = attend(
                len_ref, s, q_s, k_s, v_s, tk_s, tv_s
            )
        own_part(p).start()
        their_part(p, c).start()

    @pl.loop(0, PAIRS)
    def _(p):
        own_part(p).wait()
        their_part(p, c).wait_send()
        their_part(p, 1 - c).wait_recv()

    hand_over(xs, 0).wait_send()
    hand_over(ts, 1).wait_send()
    sent(0)
    sent(1)

    @pl.loop(0, STEPS)
    def _(a):
        sent(2, a)

    pltpu.make_async_copy(others, others, a2a_s).wait()


def fused(src, blk, lens, u, caps, img, ig, tg, tm):
    hbm = pl.BlockSpec(memory_space=pl.ANY)
    vmem = pl.BlockSpec(memory_space=pltpu.VMEM)
    smem = pl.BlockSpec(memory_space=pltpu.SMEM)
    dma = pltpu.SemaphoreType.DMA
    head = pltpu.VMEM((2 * ROWS, 128), bf16)
    return pl.pallas_call(
        fused_kernel,
        out_shape=jax.ShapeDtypeStruct((ROWS, HW), bf16),
        in_specs=[smem, smem, smem, hbm, hbm, hbm, vmem, vmem, vmem],
        out_specs=hbm,
        scratch_shapes=[
            pltpu.VMEM((9, 3, 4, 4, 4, PADF, 128), bf16),
            pltpu.VMEM((128, FEAT, 384), bf16),
            pltpu.VMEM((64, 4, PADF, 128), bf16),
            pltpu.VMEM((64, 4, PADF, 128), bf16),
            pltpu.VMEM((ROWS, D), bf16),
            pltpu.VMEM((2, ROWS, DP), bf16),
            pltpu.VMEM((2, ROWS, DP), bf16),
            pltpu.VMEM((DP // 128, 256, 128), bf16),
            pltpu.VMEM((PAIRS, 2, ROWS, 128), bf16),
            head, head, head, head, head,
            dma((4,)),
            dma((2, 3, 4)), dma((2, 3, 4)),
            dma((9, 3, 4)), dma((9, 3, 4)),
            dma, dma,
            dma((2,)), dma((2,)),
            dma((PAIRS,)), dma((PAIRS,)), dma((PAIRS,)),
        ],
        compiler_params=pltpu.CompilerParams(
            collective_id=0, has_side_effects=True, vmem_limit_bytes=63 << 20
        ),
        name="joint_attention",
    )(src, blk, lens, u, caps, img, ig, tg, tm)


def chip_weights(image_qkv, text_kv, core):
    wi = image_qkv.reshape(19, 3, 2, PAIRS, 128)
    wt = text_kv.reshape(19, 2, 2, PAIRS, 128)
    w = jnp.concatenate([wi, wt], axis=1).transpose(2, 3, 1, 0, 4)
    w = w.reshape(2, 25, 19, 128)
    w = jnp.where(
        core == 0,
        jnp.pad(w, ((0, 0), (0, 0), (0, 21), (0, 0))),
        jnp.pad(w, ((0, 0), (0, 0), (19, 2), (0, 0))),
    )
    mine = jnp.where(core == 0, w[0], w[1])
    other = jnp.where(core == 0, w[1], w[0])
    return mine + lax.ppermute(other, "c", [(0, 1), (1, 0)])


def shards(
    image_tokens, image_gain, caption_states, text_gain, lengths, assign, image_qkv, text_kv
):
    core = lax.axis_index("c")
    chip = lax.axis_index(("yl", "z", "x"))
    u = chip_weights(image_qkv, text_kv, core)
    u = jnp.pad(u, ((0, 2), (0, 0), (0, 0))).reshape(9, 3, PADF, 128)

    places = jnp.arange(128, dtype=jnp.int32)
    match = assign[0][:, None] == places[None, :]
    inverse = jnp.sum(jnp.where(match, places[:, None], 0), axis=0)
    ordered = jnp.sum(jnp.where(match, lengths[0][:, None], 0), axis=0)
    pair_src = inverse.reshape(64, 2)
    first = (ordered.reshape(64, 2)[:, :1] + 127) // 128
    slot = jnp.arange(4, dtype=jnp.int32)[None, :]
    own = slot < first
    src = jnp.where(own, pair_src[:, :1], pair_src[:, 1:]).reshape(256)
    blk = jnp.clip(jnp.where(own, slot, 3 - slot), 0, 2).reshape(256)
    lens = lax.dynamic_slice_in_dim(ordered, chip * 4, 4, 0)

    def spread_row(v):
        return jnp.pad(v.reshape(CHIPS, FEAT), ((0, 0), (0, 2))).reshape(1, DP)

    out = fused(
        src, blk, lens, u,
        jnp.transpose(caption_states, (0, 2, 1)),
        image_tokens.reshape(ROWS, D),
        image_gain.reshape(1, D),
        spread_row(text_gain),
        spread_row(jnp.ones((D,), f32)),
    )
    return out.reshape(2, 256, HW)


def solution(mesh):
    fine = Mesh(mesh.devices.reshape(2, 2, 4, 4, 2), AXES)
    full = P(AXES)
    placed = (
        P(AXES, None, None),
        P(),
        P("yh", None, SHARD_AXES),
        P(),
        P("yh", None),
        P("yh", None),
        P(AXES, None),
        P(AXES, None),
    )
    return jax.shard_map(
        shards,
        mesh=fine,
        in_specs=placed,
        out_specs=P(AXES, None, None),
        check_vma=False,
    )
```
